256 devices in a mesh: chan: 64 (over z, x_hi, y), tile: 4 (over x_lo, core).
Axes of the slice: x: 4 (x_hi: 2, x_lo: 2; x = x_hi * 2 + x_lo), y: 4, z: 8, core: 2. Of those that a mesh axis runs over, the one named last changes fastest.
Arguments:
- voltages: bfloat16 [2048, 276480], P(('chan', 'tile')), may hold values from -6 to 6
- tile_order: int32 [2048], replicated, may hold values from 0 to 2047, each once
- beam_index: int32 [512, 1024], replicated, may hold values from 0 to 127
- beam_table: float32 [2, 64, 128], P(None, 'chan'), may hold values from -0.1875 to 0.1875
Outputs:
- visibility: float32 [2, 64, 2048, 2048], P(None, 'chan', 'tile')
- beams: float32 [2, 64, 2, 128, 512], P(None, 'chan', None, None, 'tile')
The draws below stay inside these ranges and needn't reach their ends.
Inputs may be any that keep to these rules, and one draw needn't show every extreme that they name: `tile_order`: each input appears once.
All inputs are finite; a program needn't handle non-finite values.
Results may differ from the reference program's by a relative error of at most 0.0068.
Values may be sent and summed in bfloat16 or wider, within the bound.
A program may use at most 128 MiB of HBM per device.

```python
import math
import jax
import jax.numpy as jnp
from jax import lax

INPUTS = 2048
FFT_LEN = 2048
TAPS = 8
BEAMS = 512
NTAB = 128
BAND_START = 256
SPECTRA = 128
CHANNELS = 64
ANTENNAS = 1024
SAMPLES = 276480


def set_ends(values, stream_key, least, high):
    place = [jax.random.randint(jax.random.fold_in(stream_key, axis), (), 0, length) for axis, length in enumerate(values.shape)]
    main_axis = values.shape.index(max(values.shape))
    neighbour = place[:main_axis] + [(place[main_axis] + 1) % values.shape[main_axis]] + place[main_axis + 1:]
    return values.at[tuple(place)].set(least).at[tuple(neighbour)].set(high)


def steps_of(stream_key, shape, shards, smallest, largest):
    def one(position, blocks):
        draws = jax.random.uniform(jax.random.fold_in(jax.random.fold_in(stream_key, 6), position), (blocks,), jnp.float32, smallest / len(shards), largest / len(shards))
        return jnp.repeat(jnp.exp(draws), shape[position] // blocks).reshape((-1,) + (1,) * (len(shape) - position - 1))

    factor_of = one(*shards[0])
    for cut in shards[1:]:
        factor_of = factor_of * one(*cut)
    return factor_of


def noise(key, extent, deviation, most, pieces=(), held_as=jnp.bfloat16):
    result = jax.random.normal(key, extent, jnp.float32) * deviation
    if len(pieces) > 0:
        result = steps_of(key, extent, pieces, -0.22, 0.18) * result
    return jnp.clip(result, min=-most, max=most).astype(held_as)


def setup_inputs(seed: int = 0) -> dict:
    splits = jax.random.split(jax.random.key(seed), 5)
    voltages = noise(splits[0], (INPUTS, SAMPLES), 1.0, 6.0, ((0, 256),))
    tile_order = jax.random.permutation(splits[1], INPUTS).astype(jnp.int32)
    beam_index = set_ends(jax.random.randint(splits[2], (BEAMS, ANTENNAS), 0, NTAB), jax.random.fold_in(splits[2], 1), 0, NTAB - 1).astype(jnp.int32)
    beam_table = noise(splits[3], (2, CHANNELS, NTAB), ANTENNAS ** -0.5, 0.1875, ((1, 64),), jnp.float32)
    return dict(voltages=voltages, tile_order=tile_order, beam_index=beam_index, beam_table=beam_table)


highest = lax.Precision.HIGHEST

def filter_taps(tap_count, frame_length):
    span_total = tap_count * frame_length
    sample_index = jnp.arange(span_total, dtype=jnp.int32).astype(jnp.float32)
    offset = (sample_index - span_total / 2.0 + 0.5) / frame_length
    window = 0.54 - 0.46 * jnp.cos(2.0 * math.pi * sample_index / (span_total - 1))
    values = jnp.sin(math.pi * offset) / (math.pi * offset) * window
    values = values / jnp.sqrt(jnp.sum(values * values) / frame_length)
    return values.reshape(tap_count, frame_length)

def fourier_table(frame_length, first_bin, channel_count):
    positions = jnp.arange(frame_length, dtype=jnp.int32)
    channel_bins = first_bin + jnp.arange(channel_count, dtype=jnp.int32)
    phases = positions[:, None] * channel_bins[None, :] % frame_length
    angles = phases.astype(jnp.float32) * (2.0 * math.pi / frame_length)
    norm_scale = 1.0 / math.sqrt(frame_length)
    table = jnp.concatenate([jnp.cos(angles), -jnp.sin(angles)], axis=1) * norm_scale
    return table.astype(jnp.bfloat16)

def reference(voltages, tile_order, beam_index, beam_table):
    tap_table = filter_taps(TAPS, FFT_LEN)
    fourier = fourier_table(FFT_LEN, BAND_START, CHANNELS)
    input_groups = voltages.reshape(INPUTS // 64, 64, SAMPLES)

    def channelize(voltage_group):
        frames = voltage_group.astype(jnp.float32).reshape(64, SPECTRA + TAPS - 1, FFT_LEN)
        filtered = jnp.zeros((64, SPECTRA, FFT_LEN), jnp.float32)
        for tap_index in range(TAPS):
            filtered = filtered + tap_table[tap_index] * frames[:, tap_index:tap_index + SPECTRA, :]
        filtered = filtered.astype(jnp.bfloat16).reshape(64 * SPECTRA, FFT_LEN)
        spectrum = jnp.dot(filtered, fourier, preferred_element_type=jnp.float32)
        spectrum = spectrum.reshape(64, SPECTRA, 2, CHANNELS)
        return jnp.transpose(spectrum, (2, 0, 1, 3)).astype(jnp.bfloat16)
    channelized = lax.map(channelize, input_groups)
    spectra = jnp.transpose(channelized, (4, 1, 0, 2, 3)).reshape(CHANNELS, 2, INPUTS, SPECTRA)
    tables = jnp.transpose(beam_table, (1, 0, 2))

    def correlate(inputs_one):
        spectra_one, table_one = inputs_one
        real_part = spectra_one[0]
        imag_part = spectra_one[1]
        chosen_real = real_part[tile_order]
        chosen_imag = imag_part[tile_order]

        def product(left, right):
            return jnp.dot(left, right.T, preferred_element_type=jnp.float32)
        vis_real = (product(chosen_real, real_part) + product(chosen_imag, imag_part)) / SPECTRA
        vis_imag = (product(chosen_imag, real_part) - product(chosen_real, imag_part)) / SPECTRA
        weight_real = table_one[0].astype(jnp.bfloat16)[beam_index]
        weight_imag = table_one[1].astype(jnp.bfloat16)[beam_index]
        antenna_real = real_part.reshape(ANTENNAS, 2, SPECTRA)
        antenna_imag = imag_part.reshape(ANTENNAS, 2, SPECTRA)

        def combine(weight_part, data_part):
            return jnp.einsum('ba,aps->psb', weight_part.astype(jnp.float32), data_part.astype(jnp.float32), precision=highest)
        beam_real = combine(weight_real, antenna_real) - combine(weight_imag, antenna_imag)
        beam_imag = combine(weight_real, antenna_imag) + combine(weight_imag, antenna_real)
        return (jnp.stack([vis_real, vis_imag], axis=0), jnp.stack([beam_real, beam_imag], axis=0))
    vis_all, beam_all = lax.map(correlate, (spectra, tables))
    return (jnp.transpose(vis_all, (1, 0, 2, 3)), jnp.transpose(beam_all, (1, 0, 2, 3, 4)))
```

```python
import functools
import math

import jax
import jax.numpy as jnp
import numpy as np
from jax import lax
from jax.experimental import pallas as pl
from jax.experimental.pallas import tpu as pltpu

FRAME_BLOCKS = ((0, 272), (272, 544), (544, 816), (816, 1080))
SENT = ((0, 2, 6, 4), (1, 7, 3, 5))
SCHEDULE = "f4 p0 f5 p1 d0 f6 p2 d1 f7 p3 d2 p4 d3 p5 d4 p6 d5 p7 d6 d7"
AWAITED = (0, 2, 6, 4, 1, 7, 3, 5)
MESH = pl.DeviceIdType.MESH
F32 = jnp.float32
BF16 = jnp.bfloat16


def folded_table():
    m = np.arange(16384, dtype=np.float64)
    taps = np.sinc((m - 8192 + 0.5) / 2048) * (0.54 - 0.46 * np.cos(2 * np.pi * m / 16383))
    taps = taps / np.sqrt(np.sum(taps * taps) / 2048)
    taps = taps.reshape(4, 2, 2048).astype(np.float32)
    phases = (np.arange(2048)[:, None] * (256 + np.arange(64))[None, :]) % 2048
    angles = phases * (2 * np.pi / 2048)
    table = np.stack([np.cos(angles), -np.sin(angles)], axis=1) / math.sqrt(2048)
    table = table.astype(np.float32).astype(BF16).astype(np.float32)
    table = table.reshape(2048, 2, 4, 2, 8)
    folded = taps[:, :, :, None, None, None, None] * table[None, None]
    folded = folded.transpose(5, 2, 0, 1, 3, 4, 6)
    return folded.reshape(2, 2048, 512).astype(BF16)


def first_kernel(
    x_hbm, w_hbm, order_hbm, index_hbm, table_hbm,
    all_ref, total_ref,
    x_ref, w_ref, index_ref, order_ref, table_ref, products, halves, msg_r, msg_i, message, select_ref,
    load_sem, send_sem, a_sem, xs_sem, xr_sem, cs_sem, cr_sem, ds_sem, dr_sem,
):
    chan = lax.axis_index("chan")
    tile = lax.axis_index("tile")
    z = chan // 8
    xh = (chan // 4) % 2
    y = chan % 4
    tile_x = (tile + 2) % 4
    tile_c = tile + 1 - 2 * (tile % 2)
    tile_d = tile_x + 1 - 2 * (tile_x % 2)

    def peer(dz, dx, dy):
        other = ((z + dz) % 8) * 8 + ((xh + dx) % 2) * 4 + (y + dy) % 4
        return (other, tile_x if dx else tile)

    frame_loads = [
        pltpu.make_async_copy(x_hbm.at[lo:hi], x_ref.at[lo:hi], load_sem.at[6 + n])
        for n, (lo, hi) in enumerate(FRAME_BLOCKS)
    ]
    small_loads = [
        pltpu.make_async_copy(order_hbm, order_ref, load_sem.at[3]),
        pltpu.make_async_copy(table_hbm, table_ref, load_sem.at[4]),
        pltpu.make_async_copy(index_hbm.at[pl.ds(tile * 128, 128)], index_ref, load_sem.at[5]),
    ]
    table_loads = [
        pltpu.make_async_copy(w_hbm.at[(z + part) % 2], w_ref.at[part], load_sem.at[part])
        for part in range(2)
    ]
    table_loads[0].start()
    frame_loads[0].start()
    frame_loads[1].start()

    barrier = pltpu.get_barrier_semaphore()

    for dz in (4, 3, 5, 2, 6, 1, 7, 0):
        for dx in range(2):
            for dy in range(4):
                if dz or dx or dy:
                    pl.semaphore_signal(
                        barrier, inc=1, device_id=peer(dz, dx, dy), device_id_type=MESH
                    )
    for near in (tile_x, tile_c):
        pl.semaphore_signal(barrier, inc=1, device_id=(chan, near), device_id_type=MESH)

    after = (
        (frame_loads[2],),
        (frame_loads[3],),
        (table_loads[1],),
        small_loads,
    )

    def channelize(part):
        for n, (lo, hi) in enumerate(FRAME_BLOCKS):
            if part == 0:
                frame_loads[n].wait()
                for load in after[n]:
                    load.start()
            products[lo:hi] = jnp.dot(x_ref[lo:hi], w_ref[part], preferred_element_type=F32)
        pairs = products[0:1032, 0:128]
        for q in range(1, 4):
            pairs = pairs + products[16 * q : 16 * q + 1032, 128 * q : 128 * q + 128]
        halves[...] = pairs[0:1024] + pltpu.roll(pairs[8:1032], 64, 1)
        for i in range(8):
            turned = halves[pl.ds(i, 128, stride=8), :].T
            msg_r[pl.ds(i, 32, stride=8), :] = turned[0:32]
            msg_i[pl.ds(i, 32, stride=8), :] = turned[32:64]
        rows = pl.ds(256 * part, 256)
        message[rows, 0:128] = msg_r[...].astype(BF16)
        message[rows, 128:256] = msg_i[...].astype(BF16)

    def send_planes(part, offsets):
        for dz in offsets:
            plane_row = 256 * part + 64 * (((z + dz) % 8) // 2)
            for dx in range(2):
                for dy in range(4):
                    to = peer(dz, dx, dy)
                    row = pl.multiple_of(plane_row + 32 * ((xh + dx) % 2) + 8 * ((y + dy) % 4), 8)
                    source = message.at[pl.ds(row, 8)]
                    group = a_sem.at[chan // 4]
                    if dz or dx or dy:
                        pltpu.make_async_remote_copy(
                            src_ref=source,
                            dst_ref=all_ref.at[chan, tile],
                            send_sem=send_sem,
                            recv_sem=group,
                            device_id=to,
                            device_id_type=MESH,
                        ).start()
                    else:
                        pltpu.make_async_copy(source, all_ref.at[chan, tile], group).start()

    table_loads[0].wait()
    channelize(0)
    pl.semaphore_wait(barrier, 65)
    send_planes(0, SENT[0])
    table_loads[1].wait()
    channelize(1)
    send_planes(1, SENT[1])

    def plane(step):
        return (z + 8 - AWAITED[step]) % 8

    def chunk(zz, xx, t):
        return all_ref.at[pl.ds(zz * 8 + xx * 4, 4), t]

    def origin(xx, t):
        return (t + 2 * ((xx + xh) % 2)) % 4

    def copy_to(zz, xx, t, to, s_sem, r_sem):
        return pltpu.make_async_remote_copy(
            src_ref=chunk(zz, xx, t),
            dst_ref=chunk(zz, xx, t),
            send_sem=s_sem,
            recv_sem=r_sem.at[zz * 2 + xx],
            device_id=(chan, to),
            device_id_type=MESH,
        )

    def forward(step):
        zz = plane(step)
        for xx in range(2):
            t = origin(xx, tile)
            got = chunk(zz, xx, t)
            pltpu.make_async_copy(got, got, a_sem.at[zz * 2 + xx]).wait()
            copy_to(zz, xx, t, tile_x, xs_sem, xr_sem).start()
            copy_to(zz, xx, t, tile_c, cs_sem, cr_sem).start()

    for step in range(4):
        forward(step)

    for load in small_loads:
        load.wait()
    lane = lax.broadcasted_iota(jnp.int32, (128, 128), 1)
    lane_f = lane.astype(F32)
    for q in range(4):
        row = order_ref[pl.ds(tile * 4 + q, 1), :].astype(F32)
        wanted = jnp.broadcast_to(row, (128, 128)).T
        for block in range(16):
            hot = jnp.where(wanted == lane_f + 128.0 * block, 1.0, 0.0)
            column = 128 * (block % 2)
            select_ref[block // 2, 128 * q : 128 * q + 128, column : column + 128] = hot.astype(BF16)
    parts = [
        jnp.broadcast_to(table_ref[p].astype(BF16).astype(F32), (128, 128)) for p in range(2)
    ]
    even = lane % 2 == 0
    for block in range(16):
        a = 128 * (block // 2)
        spread = jnp.take_along_axis(
            index_ref[:, a : a + 128], lane // 2 + 64 * (block % 2), axis=1, mode="promise_in_bounds"
        )
        column = 128 * (block % 2)
        for p in range(2):
            value = jnp.take_along_axis(parts[p], spread, axis=1, mode="promise_in_bounds")
            for pol in range(2):
                kept = jnp.where(even if pol == 0 else ~even, value, 0.0)
                base = 512 + 256 * pol + 128 * p
                select_ref[block // 2, base : base + 128, column : column + 128] = kept.astype(BF16)

    def pass_on(step):
        zz = plane(step)
        for xx in range(2):
            t = origin(xx, tile_x)
            copy_to(zz, xx, t, tile_x, xs_sem, xr_sem).wait_recv()
            copy_to(zz, xx, t, tile_c, ds_sem, dr_sem).start()

    def finish(step):
        zz = plane(step)
        for xx in range(2):
            copy_to(zz, xx, origin(xx, tile_c), tile_c, cs_sem, cr_sem).wait_recv()
            copy_to(zz, xx, origin(xx, tile_d), tile_c, ds_sem, dr_sem).wait_recv()
        block = all_ref[pl.ds(zz * 8, 8)].reshape(256, 256)
        product = jnp.dot(select_ref[zz], block, preferred_element_type=F32)
        total_ref[...] = product if step == 0 else total_ref[...] + product

    stages = {"f": forward, "p": pass_on, "d": finish}
    for stage in SCHEDULE.split():
        stages[stage[0]](int(stage[1]))

    for sent in (xs_sem, cs_sem, ds_sem):
        pltpu.make_async_remote_copy(
            src_ref=all_ref.at[:, 0],
            dst_ref=all_ref.at[:, 0],
            send_sem=sent,
            recv_sem=send_sem,
            device_id=(chan, tile_x),
            device_id_type=MESH,
        ).wait_send()
    pltpu.make_async_remote_copy(
        src_ref=message.at[0:504],
        dst_ref=message.at[0:504],
        send_sem=send_sem,
        recv_sem=send_sem,
        device_id=(chan, tile_x),
        device_id_type=MESH,
    ).wait_send()


def second_kernel(all_ref, total_ref, vis_hbm, beam_ref, left, blocks, sems):
    rows = total_ref[0:512]
    left[0:512] = rows.astype(BF16)
    left[512:1024, 0:128] = rows[:, 128:256].astype(BF16)
    left[512:1024, 128:256] = (-rows[:, 0:128]).astype(BF16)
    copies = []
    for n in range(8):
        product = lax.dot_general(
            left[...], all_ref[256 * n : 256 * n + 256], (((1,), (1,)), ((), ())),
            preferred_element_type=F32,
        )
        blocks[n] = (product * (1.0 / 128.0)).reshape(2, 512, 256)
        copy = pltpu.make_async_copy(
            blocks.at[n], vis_hbm.at[:, 0, :, pl.ds(256 * n, 256)], sems.at[n]
        )
        copy.start()
        copies.append(copy)
    for pol in range(2):
        direct = total_ref[512 + 256 * pol : 640 + 256 * pol]
        crossed = total_ref[640 + 256 * pol : 768 + 256 * pol]
        beam_ref[0, 0, pol] = (direct[:, 0:128] - crossed[:, 128:256]).T
        beam_ref[1, 0, pol] = (direct[:, 128:256] + crossed[:, 0:128]).T
    for copy in copies:
        copy.wait()


def body(voltages, tile_order, beam_index, beam_table):
    frames = voltages.reshape(8, 135, 2048).transpose(1, 0, 2).reshape(1080, 2048)
    vmem = pl.BlockSpec(memory_space=pltpu.VMEM)
    anywhere = pl.BlockSpec(memory_space=pltpu.HBM)
    dma = pltpu.SemaphoreType.DMA
    everything, total = pl.pallas_call(
        first_kernel,
        name="channelize_exchange",
        out_shape=(
            jax.ShapeDtypeStruct((64, 4, 8, 256), BF16),
            jax.ShapeDtypeStruct((1024, 256), F32),
        ),
        in_specs=[anywhere] * 5,
        out_specs=(vmem, vmem),
        scratch_shapes=[
            pltpu.VMEM((1080, 2048), BF16),
            pltpu.VMEM((2, 2048, 512), BF16),
            pltpu.VMEM((128, 1024), jnp.int32),
            pltpu.VMEM((16, 128), jnp.int32),
            pltpu.VMEM((2, 1, 128), F32),
            pltpu.VMEM((1080, 512), F32),
            pltpu.VMEM((1024, 128), F32),
            pltpu.VMEM((256, 128), F32),
            pltpu.VMEM((256, 128), F32),
            pltpu.VMEM((512, 256), BF16),
            pltpu.VMEM((8, 1024, 256), BF16),
            dma((10,)), dma(()), dma((16,)),
            dma(()), dma((16,)), dma(()), dma((16,)), dma(()), dma((16,)),
        ],
        compiler_params=pltpu.CompilerParams(
            collective_id=0, has_side_effects=True, vmem_limit_bytes=32 * 2**20
        ),
    )(*[
        pltpu.with_memory_space_constraint(operand, pltpu.HBM)
        for operand in (
            frames, jnp.asarray(folded_table()), tile_order.reshape(16, 128), beam_index, beam_table
        )
    ])
    return pl.pallas_call(
        second_kernel,
        name="correlate",
        out_shape=(
            jax.ShapeDtypeStruct((2, 1, 512, 2048), F32),
            jax.ShapeDtypeStruct((2, 1, 2, 128, 128), F32),
        ),
        in_specs=[vmem, vmem],
        out_specs=(anywhere, vmem),
        scratch_shapes=[
            pltpu.VMEM((1024, 256), BF16),
            pltpu.VMEM((8, 2, 512, 256), F32),
            dma((8,)),
        ],
        compiler_params=pltpu.CompilerParams(vmem_limit_bytes=24 * 2**20),
    )(everything.reshape(2048, 256), total)


def solution(mesh):
    from jax.sharding import PartitionSpec as P

    return jax.shard_map(
        body,
        mesh=mesh,
        in_specs=(P(("chan", "tile"), None), P(), P(), P(None, "chan", None)),
        out_specs=(P(None, "chan", "tile", None), P(None, "chan", None, None, "tile")),
        check_vma=False,
    )
```
